128 devices in a mesh: gx: 16 (over y, z), yz: 8 (over x, core).
Axes of the slice: x: 4, y: 4, z: 4, core: 2. Of those that a mesh axis runs over, the one named last changes fastest.
Arguments:
- right_side: float32 [64, 256, 512], P('gx', 'yz'), may hold values from -5 to 5
- phase: int32 [64, 256, 512], P('gx', 'yz'), may hold values 0 or 1
- pressure_guess: float32 [64, 256, 512], P('gx', 'yz'), may hold values from -6 to 6
Outputs:
- pressure: float32 [64, 256, 512], P('gx', 'yz')
- residual: float32 [64, 256, 512], P('gx', 'yz')
The draws below stay inside these ranges and needn't reach their ends.
All inputs are finite; a program needn't handle non-finite values. No bound on the sum of `phase` on one device may be relied on, other than what follows from the above.
Results may differ from the reference program's by a relative error of at most 0.0003.
Values sent between devices are 32-bit elements; how exact they have to be, the bound alone decides.
A program may use at most 128 MiB of HBM per device.

```python
import jax
import jax.numpy as jnp
from jax import lax

NZ = 512
SWEEPS = 2
BOTTOM_SWEEPS = 4
NX = 64
NY = 256


def draw_right_side(key, part):
    extent = (NX, NY, NZ)
    return jnp.clip(jax.random.normal(key, extent, jnp.float32), -5.0, 5.0)


def place_ends(entries, own_key, low, high):
    longest = entries.shape.index(max(entries.shape))
    spots = []
    for shift in (0, 1):
        where = [jax.random.randint(jax.random.fold_in(own_key, axis), (), 0, length) for axis, length in enumerate(entries.shape)]
        where[longest] = (where[longest] + shift) % entries.shape[longest]
        spots.append(tuple(where))
    return entries.at[spots[0]].set(low).at[spots[1]].set(high)


def steps_of(stream_key, dims, shards, low, largest):
    def one(position, blocks):
        draws = jax.random.uniform(jax.random.fold_in(jax.random.fold_in(stream_key, 6), position), (blocks,), jnp.float32, low / len(shards), largest / len(shards))
        return jnp.repeat(jnp.exp(draws), dims[position] // blocks).reshape((-1,) + (1,) * (len(dims) - position - 1))

    gain = one(*shards[0])
    for cut in shards[1:]:
        gain = gain * one(*cut)
    return gain


def gaussian(key, dims, deviation, reach, cuts=(), held_as=jnp.bfloat16):
    gain = steps_of(key, dims, cuts, -0.22, 0.18) if cuts else 1.0
    array = jax.random.normal(key, dims, jnp.float32) * deviation * gain
    return jnp.minimum(jnp.maximum(array, -reach), reach).astype(held_as)


def setup_inputs(seed: int = 0) -> dict:
    seeds = jax.random.split(jax.random.key(seed), 4)
    return {
        "right_side": draw_right_side(jax.random.fold_in(seeds[3], 71), 0),
        "phase": place_ends((jax.random.randint(seeds[1], (NX, NY, NZ), 0, 4) < 1).astype(jnp.int32), jax.random.fold_in(seeds[1], 1), 0, 1),
        "pressure_guess": gaussian(seeds[2], (NX, NY, NZ), 1.0, 6.0, ((0, 16), (1, 8)), jnp.float32),
    }


def harmonic(left, right):
    total = left + right
    safe = jnp.where(total > 0, total, 1.0)
    return jnp.where(total > 0, 2.0 * left * right / safe, 0.0)


def coefficients(padded):
    faces_x = harmonic(padded[1:], padded[:-1])
    faces_y = harmonic(padded[:, 1:], padded[:, :-1])
    centre = padded[1:-1, 1:-1]
    faces_z = harmonic(centre[:, :, 1:], centre[:, :, :-1])
    zero_plane = jnp.zeros_like(centre[:, :, :1])
    x_lower = faces_x[:-1, 1:-1]
    x_upper = faces_x[1:, 1:-1]
    y_lower = faces_y[1:-1, :-1]
    y_upper = faces_y[1:-1, 1:]
    z_lower = jnp.concatenate([zero_plane, faces_z], axis=2)
    z_upper = jnp.concatenate([faces_z, 2.0 * centre[:, :, -1:]], axis=2)
    diagonal = x_lower + x_upper + y_lower + y_upper + z_lower + z_upper
    diagonal = jnp.where(diagonal > 0, diagonal, 1.0)
    return (x_lower, x_upper, y_lower, y_upper, z_lower, z_upper, diagonal)


def parity_of(extent, start_x, start_y):
    index_x = lax.broadcasted_iota(jnp.int32, extent, 0) + start_x
    index_y = lax.broadcasted_iota(jnp.int32, extent, 1) + start_y
    index_z = lax.broadcasted_iota(jnp.int32, extent, 2)
    return (index_x + index_y + index_z) % 2


def neighbours(padded, coeffs):
    centre = padded[1:-1, 1:-1]
    zero_plane = jnp.zeros_like(centre[:, :, :1])
    lower_z = jnp.concatenate([zero_plane, centre[:, :, :-1]], axis=2)
    upper_z = jnp.concatenate([centre[:, :, 1:], zero_plane], axis=2)
    beside_all = coeffs[0] * padded[:-2, 1:-1] + coeffs[1] * padded[2:, 1:-1]
    beside_all = beside_all + coeffs[2] * padded[1:-1, :-2] + coeffs[3] * padded[1:-1, 2:]
    beside_all = beside_all + coeffs[4] * lower_z + coeffs[5] * upper_z
    return beside_all, centre


def colour_pass(padded, source, coeffs, parity, colour):
    beside_all, centre = neighbours(padded, coeffs)
    updated = (source + beside_all) / coeffs[6]
    return jnp.where(parity == colour, updated, centre)


def residual_of(padded, source, coeffs):
    beside_all, centre = neighbours(padded, coeffs)
    return source - (coeffs[6] * centre - beside_all)


def restrict_sum(field):
    size_x, size_y, size_z = field.shape
    return 0.5 * field.reshape(size_x // 2, 2, size_y // 2, 2, size_z // 2, 2).sum(axis=(1, 3, 5))


def restrict_mean(field):
    size_x, size_y, size_z = field.shape
    return 0.125 * field.reshape(size_x // 2, 2, size_y // 2, 2, size_z // 2, 2).sum(axis=(1, 3, 5))


def inject(field):
    return jnp.repeat(jnp.repeat(jnp.repeat(field, 2, axis=0), 2, axis=1), 2, axis=2)


def pad_xy(field):
    return jnp.pad(field, ((1, 1), (1, 1), (0, 0)))


def smooth_whole(field, source, coeffs, parity, sweeps):
    for _ in range(sweeps):
        field = colour_pass(pad_xy(field), source, coeffs, parity, 0)
        field = colour_pass(pad_xy(field), source, coeffs, parity, 1)
    return field


def reference(right_side, phase, pressure_guess):
    mobility = 1.0 + 999.0 * phase.astype(jnp.float32)
    coeffs_zero = coefficients(pad_xy(mobility))
    parity_zero = parity_of(mobility.shape, 0, 0)
    pressure = smooth_whole(pressure_guess, right_side, coeffs_zero, parity_zero, SWEEPS)
    fine_res = residual_of(pad_xy(pressure), right_side, coeffs_zero)
    source_one = restrict_sum(fine_res)
    mobility_one = restrict_mean(mobility)
    coeffs_one = coefficients(pad_xy(mobility_one))
    parity_one = parity_of(mobility_one.shape, 0, 0)
    coarse_one = smooth_whole(jnp.zeros_like(source_one), source_one, coeffs_one, parity_one, SWEEPS)
    res_one = residual_of(pad_xy(coarse_one), source_one, coeffs_one)
    source_two = restrict_sum(res_one)
    mobility_two = restrict_mean(mobility_one)
    coeffs_two = coefficients(pad_xy(mobility_two))
    parity_two = parity_of(mobility_two.shape, 0, 0)
    coarse_two = smooth_whole(jnp.zeros_like(source_two), source_two, coeffs_two, parity_two, BOTTOM_SWEEPS)
    coarse_one = smooth_whole(coarse_one + inject(coarse_two), source_one, coeffs_one, parity_one, SWEEPS)
    pressure = smooth_whole(pressure + inject(coarse_one), right_side, coeffs_zero, parity_zero, SWEEPS)
    residual = residual_of(pad_xy(pressure), right_side, coeffs_zero)
    return (pressure, residual)
```

```python
import functools

import jax
import jax.numpy as jnp
import numpy as np
from jax import lax
from jax.experimental import pallas as pl
from jax.experimental.pallas import tpu as pltpu
from jax.sharding import PartitionSpec as P

MESH = pl.DeviceIdType.MESH
F32 = jnp.float32
LANES = 128
SUB = 8
PAD2 = 3
MIXED = np.float32(2000.0) / np.float32(1001.0)
NEAR = [(a, b) for a in (-1, 0, 1) for b in (-1, 0, 1) if (a, b) != (0, 0)]


def lanes_of(shape):
    return lax.broadcasted_iota(jnp.int32, shape, len(shape) - 1)


def roll(value, shift, axis):
    size = value.shape[axis]
    return pltpu.roll(value, shift % size, axis)


def split_lanes(tiles):
    shape = tiles[0].shape
    lane = lanes_of(shape)
    block = lane // 32
    within = lane % 32
    parts = [
        jnp.take_along_axis(tiles[t], 4 * within + (block + 4 - t) % 4, axis=1) for t in range(4)
    ]
    out = []
    for k in range(4):
        pick = parts[(3 - k) % 4]
        for b in (2, 1, 0):
            pick = jnp.where(block == b, parts[(b - k) % 4], pick)
        out.append(pick if k == 0 else roll(pick, -32 * k, 1))
    return out


def join_lanes(quarters):
    shape = quarters[0].shape
    lane = lanes_of(shape)
    block = lane // 32
    turned = [quarters[k] if k == 0 else roll(quarters[k], 32 * k, 1) for k in range(4)]
    out = []
    for t in range(4):
        pick = turned[(3 - t) % 4]
        for b in (2, 1, 0):
            pick = jnp.where(block == b, turned[(b - t) % 4], pick)
        out.append(jnp.take_along_axis(pick, ((lane % 4 + t) % 4) * 32 + lane // 4, axis=1))
    return out


def planes(low, high, body):
    count = high - low
    if count % 2 == 0 and count > 2:

        def pair(i, carry):
            body(low + 2 * i, low % 2)
            body(low + 2 * i + 1, (low + 1) % 2)
            return carry

        lax.fori_loop(0, count // 2, pair, 0)
    else:
        for x in range(low, high):
            body(x, x % 2)


class Level:
    def __init__(self, rows, pairs, refs, face):
        self.rows, self.pairs, self.face = rows, pairs, face
        self.v, self.s, self.m, self.cx, self.cy, self.cz, self.cyl, self.czl, self.d, self.inv = refs

    def bit(self, c, par, r):
        return (c + par + 1 + r) % 2

    def load(self, ref, x, c, par, r, start, stride):
        b = self.bit(c, par, r)
        return [ref[x, 2 * j + b, pl.ds(start, SUB, stride=stride), :] for j in range(self.pairs)]

    def z_shift_up(self, values, b):
        if b == 0:
            return values
        return values[1:] + [roll(values[0], -1, 1)]

    def z_shift_down(self, values, b):
        if b == 1:
            return values
        return [roll(values[-1], 1, 1)] + values[:-1]

    def get(self, ref, c, x, r):
        return [ref[c, x, r, j] for j in range(self.pairs)]

    def y_up(self, ref, c, x, r):
        if r < self.rows - 1:
            return self.get(ref, c, x, r + 1)
        return [roll(v, -1, 0) for v in self.get(ref, c, x, 0)]

    def y_down(self, ref, c, x, r):
        if r > 0:
            return self.get(ref, c, x, r - 1)
        return [roll(v, 1, 0) for v in self.get(ref, c, x, self.rows - 1)]

    def faces_x(self, low, high):
        def body(x, par):
            for c in (0, 1):
                for r in range(self.rows):
                    here, there = self.get(self.m, c, x, r), self.get(self.m, 1 - c, x + 1, r)
                    for j in range(self.pairs):
                        self.cx[c, x, r, j] = self.face(here[j], there[j])

        planes(low, high, body)

    def faces_yz(self, low, high):
        last = lanes_of((SUB, LANES)) == LANES - 1

        def body(x, par):
            for c in (0, 1):
                for r in range(self.rows):
                    b = self.bit(c, par, r)
                    here = self.get(self.m, c, x, r)
                    there = self.y_up(self.m, 1 - c, x, r)
                    above = self.z_shift_up(self.get(self.m, 1 - c, x, r), b)
                    for j in range(self.pairs):
                        self.cy[c, x, r, j] = self.face(here[j], there[j])
                        up = self.face(here[j], above[j])
                        if b == 1 and j == self.pairs - 1:
                            up = jnp.where(last, 0.0, up)
                        self.cz[c, x, r, j] = up

        planes(low, high, body)

    def diagonals(self, low, high):
        last = lanes_of((SUB, LANES)) == LANES - 1

        def body(x, par):
            for c in (0, 1):
                for r in range(self.rows):
                    b = self.bit(c, par, r)
                    xl, xu = self.get(self.cx, 1 - c, x - 1, r), self.get(self.cx, c, x, r)
                    yl, yu = self.y_down(self.cy, 1 - c, x, r), self.get(self.cy, c, x, r)
                    zl = self.z_shift_down(self.get(self.cz, 1 - c, x, r), b)
                    zu = self.get(self.cz, c, x, r)
                    for j in range(self.pairs):
                        if r == 0:
                            self.cyl[c, x, j] = yl[j]
                        if b == 0 and j == 0:
                            self.czl[c, x, r] = zl[j]
                        total = xl[j] + xu[j] + yl[j] + yu[j] + zl[j] + zu[j]
                        if b == 1 and j == self.pairs - 1:
                            total = total + jnp.where(last, 2.0 * self.m[c, x, r, j], 0.0)
                        total = jnp.where(total > 0, total, 1.0)
                        self.d[c, x, r, j] = total
                        self.inv[c, x, r, j] = 1.0 / total

        planes(low, high, body)

    def beside(self, c, x, par, r):
        o = 1 - c
        b = self.bit(c, par, r)
        same = self.get(self.v, o, x, r)
        parts = [
            (self.get(self.cx, o, x - 1, r), self.get(self.v, o, x - 1, r)),
            (self.get(self.cx, c, x, r), self.get(self.v, o, x + 1, r)),
            (
                self.get(self.cy, o, x, r - 1) if r else [self.cyl[c, x, j] for j in range(self.pairs)],
                self.y_down(self.v, o, x, r),
            ),
            (self.get(self.cy, c, x, r), self.y_up(self.v, o, x, r)),
        ]
        lower = self.get(self.cz, o, x, r)
        if b == 0:
            lower = [self.czl[c, x, r]] + lower[:-1]
        parts.append((lower, self.z_shift_down(same, b)))
        parts.append((self.get(self.cz, c, x, r), self.z_shift_up(same, b)))
        out = []
        for j in range(self.pairs):
            terms = [k[j] * v[j] for k, v in parts]
            out.append((terms[0] + terms[1]) + (terms[2] + terms[3]) + (terms[4] + terms[5]))
        return out

    def colour_pass(self, c, low, high):
        def body(x, par):
            for r in range(self.rows):
                total = self.beside(c, x, par, r)
                for j in range(self.pairs):
                    self.v[c, x, r, j] = (self.s[c, x, r, j] + total[j]) * self.inv[c, x, r, j]

        planes(low, high, body)

    def residual(self, c, x, par, r):
        total = self.beside(c, x, par, r)
        return [
            self.s[c, x, r, j] - (self.d[c, x, r, j] * self.v[c, x, r, j] - total[j])
            for j in range(self.pairs)
        ]


def face_fine(left, right):
    both = left * right
    return jnp.where(both > 1e5, 1000.0, jnp.where(both > 500.0, MIXED, both))


def face_coarse(left, right):
    return 2.0 * left * right / jnp.maximum(left + right, 0.5)


class Wire:
    def __init__(self, ng, ny, send, recv):
        self.ng, self.ny, self.send, self.recv, self.used = ng, ny, send, recv, 0
        self.g, self.y = lax.axis_index("gx"), lax.axis_index("yz")

    def inside(self, dg, dy):
        g, y = self.g + dg, self.y + dy
        return (g >= 0) & (g < self.ng) & (y >= 0) & (y < self.ny)

    def copy(self, src, dst, dg, dy):
        k = self.used
        self.used += 1
        made = pltpu.make_async_remote_copy(
            src_ref=src,
            dst_ref=dst,
            send_sem=self.send.at[k],
            recv_sem=self.recv.at[k],
            device_id=(self.g + dg, self.y + dy),
            device_id_type=MESH,
        )
        return (made, dst, dg, dy)

    def start(self, copies):
        for made, _, dg, dy in copies:
            pl.when(self.inside(dg, dy))(made.start)

    def arrive(self, copies, fill=0):
        for made, dst, dg, dy in copies:
            there = self.inside(-dg, -dy)
            pl.when(there)(made.wait_recv)
            if fill is not None:

                @pl.when(jnp.logical_not(there))
                def _(dst=dst):
                    dst[...] = jnp.full(dst.shape, fill, dst.dtype)

    def sent(self, copies):
        for made, _, dg, dy in copies:
            pl.when(self.inside(dg, dy))(made.wait_send)


def fine_blocks(wire, src, dst, low, high, directions):
    out = []
    for dg, dy in directions:
        if dg == 1:
            xs, xd = pl.ds(4 - high, high - low), pl.ds(3 - high, high - low)
        elif dg == -1:
            xs, xd = pl.ds(low, high - low), pl.ds(7 + low, high - low)
        else:
            xs, xd = pl.ds(0, 4), pl.ds(3, 4)
        ys, yd = ((0, 8), (40, 8)) if dy == -1 else ((24, 8), (0, 8)) if dy == 1 else ((0, 32), (8, 32))
        out.append(wire.copy(src.at[xs, pl.ds(*ys), :], dst.at[xd, pl.ds(*yd), :], dg, dy))
    return out


def middle_blocks(wire, src, dst, reach):
    out = []
    for dg in range(-3, 4):
        for dy in (-1, 0, 1):
            if (dg, dy) == (0, 0) or 2 * abs(dg) - 1 > reach:
                continue
            if abs(dg) == 3:
                xs, xd = (pl.ds(1, 1), pl.ds(0, 1)) if dg == 3 else (pl.ds(0, 1), pl.ds(11, 1))
            else:
                xs, xd = pl.ds(0, 2), pl.ds(5 - 2 * dg, 2)
            ys, yd = ((8, 8), (24, 8)) if dy == -1 else ((16, 8), (0, 8)) if dy == 1 else ((8, 16), (8, 16))
            out.append(
                wire.copy(src.at[xs, :, pl.ds(*ys), :], dst.at[xd, :, pl.ds(*yd), :], dg, dy)
            )
    return out


class Gather:
    def __init__(self, wire, src, dst):
        self.wire, self.src, self.dst = wire, src, dst
        self.first = wire.used
        self.n = wire.ng
        wire.used += self.n - 1
        self.rows = pl.ds(16, 8)
        self.along = []

    def hop(self, d, plane):
        wire = self.wire
        return pltpu.make_async_remote_copy(
            src_ref=self.src,
            dst_ref=self.dst.at[PAD2 + plane, self.rows, :],
            send_sem=wire.send.at[self.first + d - 1],
            recv_sem=wire.recv.at[self.first + d - 1],
            device_id=((wire.g + d) % self.n, wire.y),
            device_id_type=MESH,
        )

    def start(self):
        for d in range(1, self.n):
            self.hop(d, self.wire.g).start()

    def forward(self):
        for d in range(1, self.n):
            self.hop(d, (self.wire.g + self.n - d) % self.n).wait_recv()
        for dy in (-1, 1, -2, 2):
            span = pl.ds(PAD2, self.n)
            self.along.append(
                self.wire.copy(
                    self.dst.at[span, self.rows, :],
                    self.dst.at[span, pl.ds(16 - 8 * dy, 8), :],
                    0,
                    dy,
                )
            )
        self.wire.start(self.along)

    def finish(self):
        self.wire.arrive(self.along)

    def sent(self):
        for d in range(1, self.n):
            self.hop(d, self.wire.g).wait_send()
        self.wire.sent(self.along)


def kernel(
    ng, ny,
    rhs, phase, guess, p_out, r_out,
    in_phase, in_guess, in_rhs, rows_a, rows_b, rows_c,
    v0, s0, m0, cx0, cy0, cz0, cyl0, czl0, d0, inv0,
    v1, s1, m1, cx1, cy1, cz1, cyl1, czl1, d1, inv1,
    v2, s2, m2, cx2, cy2, cz2, cyl2, czl2, inv2,
    send_m1, send_s1, send_e1, wide_m1, wide_s1, wide_e1,
    send_m2, send_s2, wide_m2, wide_s2, rows_e2, rows_eb,
    got_low, got_high, last_low, last_high, far_low, far_high,
    rows_p, rows_far, p_vm, r_vm,
    local, out_sem, send, recv,
):
    wire = Wire(ng, ny, send, recv)
    g, y = wire.g, wire.y
    fine = Level(6, 2, (v0, s0, m0, cx0, cy0, cz0, cyl0, czl0, d0, inv0), face_fine)
    mid = Level(4, 1, (v1, s1, m1, cx1, cy1, cz1, cyl1, czl1, d1, inv1), face_coarse)

    own = (pl.ds(3, 4), pl.ds(8, 32))
    loads = [
        pltpu.make_async_copy(src, dst.at[own[0], own[1], :], local.at[i])
        for i, (src, dst) in enumerate(((phase, in_phase), (guess, in_guess), (rhs, in_rhs)))
    ]
    for load in loads:
        load.start()

    barrier = pltpu.get_barrier_semaphore()
    peers = [(dg, dy) for dg in range(-3, 4) for dy in (-1, 0, 1) if dy != 0 or dg == 0]
    peers = [p for p in peers if p != (0, 0)] + [(0, -2), (0, 2)]
    count = jnp.int32(ng - 1)
    for dg, dy in peers:
        there = wire.inside(dg, dy)
        count = count + there.astype(jnp.int32)

        @pl.when(there)
        def _(dg=dg, dy=dy):
            pl.semaphore_signal(barrier, inc=1, device_id=(g + dg, y + dy), device_id_type=MESH)

    for d in range(1, ng):
        pl.semaphore_signal(barrier, inc=1, device_id=((g + d) % ng, y), device_id_type=MESH)
    pl.semaphore_wait(barrier, count)

    side = [d for d in NEAR if d[0] != 0]
    phase_first = fine_blocks(wire, phase, in_phase, 0, 2, NEAR)
    guess_first = fine_blocks(wire, guess, in_guess, 0, 2, NEAR)
    rhs_first = fine_blocks(wire, rhs, in_rhs, 0, 1, NEAR)
    phase_more = fine_blocks(wire, phase, in_phase, 2, 3, side)
    rhs_more = fine_blocks(wire, rhs, in_rhs, 1, 2, side)
    for group in (phase_first, guess_first, rhs_first, phase_more, rhs_more):
        wire.start(group)

    def unpack(src, dst, low, high, first, count):
        rows = pl.ds(first, count)

        def body(x, carry):
            tiles = [src[x, rows, pl.ds(LANES * t, LANES)] for t in range(4)]
            for q, part in enumerate(split_lanes(tiles)):
                dst[x, q, rows, :] = part
            return carry

        lax.fori_loop(low, high, body, 0)

    def unpack_phase(low, high, first, count):
        rows = pl.ds(first, count)

        def body(x, carry):
            tiles = []
            for t in range(4):
                tile = in_phase[x, rows, pl.ds(LANES * t, LANES)]
                value = jnp.where(tile > 0, 1000.0, 1.0)
                tiles.append(jnp.where(tile < 0, 0.0, value))
            for q, part in enumerate(split_lanes(tiles)):
                rows_a[x, q, rows, :] = part
            return carry

        lax.fori_loop(low, high, body, 0)

    def dense(ref, rows, low, high, colours):
        def body(x, par):
            for c in colours:
                for r in range(6):
                    values = fine.load(rows, x, c, par, r, r, 6)
                    for j in range(2):
                        ref[c, x, r, j] = values[j]

        planes(low, high, body)

    loads[0].wait()
    unpack_phase(3, 7, 8, 32)
    coarsest = None
    for big in range(2):
        for q in range(2):
            for half in range(2):
                total = None
                for x in (3 + 2 * big, 4 + 2 * big):
                    for k in (0, 1):
                        for r in (2 * half, 2 * half + 1):
                            part = rows_a[x, 2 * q + k, pl.ds(8 + r, SUB, stride=4), :]
                            total = part if total is None else total + part
                total = 0.125 * total
                send_m1[big, q, pl.ds(8 + half, SUB, stride=2), :] = total
                coarsest = total if coarsest is None else coarsest + total
    coarsest = 0.125 * coarsest
    send_m2[...] = coarsest
    wide_m2[PAD2 + g, pl.ds(16, 8), :] = coarsest
    wide_m1[pl.ds(5, 2), :, pl.ds(8, 16), :] = send_m1[:, :, pl.ds(8, 16), :]

    loads[1].wait()
    unpack(in_guess, rows_b, 3, 7, 8, 32)
    loads[2].wait()
    unpack(in_rhs, rows_c, 3, 7, 8, 32)

    wire.arrive(phase_first, -1)
    for x in range(1, 9):
        if 3 <= x < 7:
            continue
        unpack_phase(x, x + 1, 0, 48)
    unpack_phase(3, 7, 0, 8)
    unpack_phase(3, 7, 40, 8)
    dense(m0, rows_a, 1, 9, (0, 1))
    fine.faces_x(1, 8)
    fine.faces_yz(2, 8)
    fine.diagonals(2, 8)

    wire.arrive(guess_first)
    unpack(in_guess, rows_b, 1, 3, 0, 48)
    unpack(in_guess, rows_b, 7, 9, 0, 48)
    unpack(in_guess, rows_b, 3, 7, 0, 8)
    unpack(in_guess, rows_b, 3, 7, 40, 8)
    dense(v0, rows_b, 1, 9, (1,))
    wire.arrive(rhs_first)
    unpack(in_rhs, rows_c, 2, 3, 0, 48)
    unpack(in_rhs, rows_c, 7, 8, 0, 48)
    unpack(in_rhs, rows_c, 3, 7, 0, 8)
    unpack(in_rhs, rows_c, 3, 7, 40, 8)
    dense(s0, rows_c, 2, 8, (0, 1))

    def sweep_one():
        fine.colour_pass(0, 2, 8)
        fine.colour_pass(1, 3, 7)

    def exchange(low, high):
        copies = [
            wire.copy(v0.at[1, pl.ds(4, 3)], low, 1, 0),
            wire.copy(v0.at[1, pl.ds(3, 3)], high, -1, 0),
        ]
        wire.start(copies)
        return copies

    def sweep_two(copies, low, high):
        wire.arrive(copies)
        v0[1, pl.ds(0, 3)] = low[...]
        v0[1, pl.ds(7, 3)] = high[...]
        fine.colour_pass(0, 1, 9)
        wire.sent(copies)
        fine.colour_pass(1, 2, 8)

    sweep_one()
    swap = exchange(got_low, got_high)
    m1_blocks = middle_blocks(wire, send_m1, wide_m1, 5)
    wire.start(m1_blocks)
    m2_all = Gather(wire, send_m2, wide_m2)
    m2_all.start()

    wire.arrive(phase_more, -1)
    unpack_phase(0, 1, 0, 48)
    unpack_phase(9, 10, 0, 48)
    dense(m0, rows_a, 0, 1, (0, 1))
    dense(m0, rows_a, 9, 10, (0, 1))
    fine.faces_x(0, 1)
    fine.faces_x(8, 9)
    fine.faces_yz(1, 2)
    fine.faces_yz(8, 9)
    fine.diagonals(1, 2)
    fine.diagonals(8, 9)
    wire.arrive(rhs_more)
    unpack(in_rhs, rows_c, 1, 2, 0, 48)
    unpack(in_rhs, rows_c, 8, 9, 0, 48)
    dense(s0, rows_c, 1, 2, (0, 1))
    dense(s0, rows_c, 8, 9, (0, 1))

    sweep_two(swap, got_low, got_high)

    for big in range(2):
        for r1 in range(3):
            total = [None, None]
            for x in (3 + 2 * big, 4 + 2 * big):
                for r in (2 * r1, 2 * r1 + 1):
                    for c in (0, 1):
                        part = fine.residual(c, x, x % 2, r)
                        for j in range(2):
                            total[j] = part[j] if total[j] is None else total[j] + part[j]
            for j in range(2):
                send_s1[big, j, pl.ds(4 + r1, SUB, stride=3), :] = 0.5 * total[j]
    s1_blocks = middle_blocks(wire, send_s1, wide_s1, 4)
    wire.start(s1_blocks)
    wide_s1[pl.ds(5, 2), :, pl.ds(8, 16), :] = send_s1[:, :, pl.ds(8, 16), :]

    for x in range(3, 7):
        for c in (0, 1):
            for r in range(6):
                b = fine.bit(c, x % 2, r)
                for j in range(2):
                    rows_p[x - 3, 2 * j + b, pl.ds(r, SUB, stride=6), :] = v0[c, x, r, j]
    far = [
        wire.copy(v0.at[1, pl.ds(5, 1)], far_low, 1, 0),
        wire.copy(v0.at[1, pl.ds(4, 1)], far_high, -1, 0),
        wire.copy(rows_p.at[:, :, pl.ds(32, 8), :], rows_far.at[:, :, pl.ds(0, 8), :], 0, 1),
        wire.copy(rows_p.at[:, :, pl.ds(8, 8), :], rows_far.at[:, :, pl.ds(40, 8), :], 0, -1),
    ]
    wire.start(far)

    wire.arrive(m1_blocks)

    def dense_mid(ref, rows, low, high, colours):
        def body(x, par):
            for c in colours:
                for r in range(4):
                    ref[c, x, r, 0] = mid.load(rows, x, c, par, r, r, 4)[0]

        planes(low, high, body)

    dense_mid(m1, wide_m1, 0, 12, (0, 1))
    mid.faces_x(0, 11)
    mid.faces_yz(1, 11)
    mid.diagonals(1, 11)
    m2_all.forward()
    v1[1] = jnp.zeros(v1.shape[1:], F32)

    def sweeps_mid():
        mid.colour_pass(0, 1, 11)
        mid.colour_pass(1, 2, 10)
        mid.colour_pass(0, 3, 9)
        mid.colour_pass(1, 4, 8)

    wire.arrive(s1_blocks)
    dense_mid(s1, wide_s1, 1, 11, (0, 1))
    sweeps_mid()
    for r2 in range(2):
        total = None
        for x in (5, 6):
            for r in (2 * r2, 2 * r2 + 1):
                for c in (0, 1):
                    part = mid.residual(c, x, x % 2, r)[0]
                    total = part if total is None else total + part
        send_s2[pl.ds(4 + r2, SUB, stride=2), :] = 0.5 * total
    s2_all = Gather(wire, send_s2.at[pl.ds(8, 8), :], wide_s2)
    s2_all.start()
    wide_s2[PAD2 + g, pl.ds(16, 8), :] = send_s2[pl.ds(8, 8), :]
    for x in (5, 6):
        for c in (0, 1):
            for r in range(4):
                b = mid.bit(c, x % 2, r)
                send_e1[x - 5, b, pl.ds(r, SUB, stride=4), :] = v1[c, x, r, 0]
    e1_blocks = middle_blocks(wire, send_e1, wide_e1, 5)
    wire.start(e1_blocks)
    wide_e1[pl.ds(5, 2), :, pl.ds(8, 16), :] = send_e1[:, :, pl.ds(8, 16), :]

    m2_all.finish()
    lane = lanes_of((SUB, LANES))
    last = lane == LANES - 1
    zero = jnp.zeros((SUB, LANES), F32)
    for x in range(PAD2):
        for r in range(4):
            for ref in (v2, m2, cx2):
                ref[x, r] = zero
                ref[PAD2 + ng + x, r] = zero

    def load_two(ref, rows):
        def body(x, carry):
            for r in range(4):
                ref[x, r] = rows[x, pl.ds(4 + r, SUB, stride=4), :]
            return carry

        lax.fori_loop(PAD2, PAD2 + ng, body, 0)

    load_two(m2, wide_m2)

    def faces_two(x, carry):
        for r in range(4):
            here = m2[x, r]
            cx2[x, r] = face_coarse(here, m2[x + 1, r])
            cy2[x, r] = face_coarse(here, m2[x, r + 1] if r < 3 else roll(m2[x, 0], -1, 0))
            up = jnp.where(last, 0.0, face_coarse(here, roll(here, -1, 1)))
            cz2[x, r] = up
            czl2[x, r] = roll(up, 1, 1)
        cyl2[x] = roll(cy2[x, 3], 1, 0)
        for r in range(4):
            yl = cy2[x, r - 1] if r else cyl2[x]
            total = cx2[x - 1, r] + cx2[x, r] + yl + cy2[x, r] + cz2[x, r] + czl2[x, r]
            total = total + jnp.where(last, 2.0 * m2[x, r], 0.0)
            inv2[x, r] = 1.0 / jnp.where(total > 0, total, 1.0)
            v2[x, r] = zero
        return carry

    lax.fori_loop(PAD2, PAD2 + ng, faces_two, 0)

    s2_all.forward()
    s2_all.finish()
    load_two(s2, wide_s2)

    def pass_two(c):
        def one(x, par):
            field = [v2[x, r] for r in range(4)]
            below, above = roll(field[3], 1, 0), roll(field[0], -1, 0)
            for r in range(4):
                yl = field[r - 1] if r else below
                yu = field[r + 1] if r < 3 else above
                total = cx2[x - 1, r] * v2[x - 1, r] + cx2[x, r] * v2[x + 1, r]
                total = total + ((cy2[x, r - 1] if r else cyl2[x]) * yl + cy2[x, r] * yu)
                total = total + (czl2[x, r] * roll(field[r], 1, 1) + cz2[x, r] * roll(field[r], -1, 1))
                value = (s2[x, r] + total) * inv2[x, r]
                hit = (lane + (par + r + c)) % 2 == 0
                v2[x, r] = jnp.where(hit, value, field[r])

        def pair(i, carry):
            one(PAD2 + 2 * i, 0)
            one(PAD2 + 2 * i + 1, 1)
            return carry

        lax.fori_loop(0, ng // 2, pair, 0)

    def sweep_of_two(i, carry):
        pass_two(0)
        pass_two(1)
        return carry

    lax.fori_loop(0, 4, sweep_of_two, 0)

    def keep_two(x, carry):
        for r in range(4):
            rows_e2[x, pl.ds(r, SUB, stride=4), :] = v2[x, r]
        return carry

    lax.fori_loop(0, ng + 2 * PAD2, keep_two, 0)

    wire.arrive(e1_blocks)
    for x in range(12):
        source = g + ((x + 1) // 2 - 3 + PAD2)
        for r in range(4):
            value = mid.load(wide_e1, x, 1, x % 2, r, r, 4)[0]
            v1[1, x, r, 0] = value + rows_e2[source, pl.ds(8 + r // 2, SUB, stride=2), :]
    sweeps_mid()
    for x in range(4, 8):
        for c in (0, 1):
            for r in range(4):
                b = mid.bit(c, x % 2, r)
                rows_eb[x - 4, b, pl.ds(r, SUB, stride=4), :] = v1[c, x, r, 0]

    wire.arrive(far[2:])
    wire.arrive(far[:2])
    wire.sent(far)
    rows_far[:, :, pl.ds(8, 32), :] = rows_p[:, :, pl.ds(8, 32), :]
    for x in range(3, 7):
        for r in range(6):
            values = fine.load(rows_far, x - 3, 1, x % 2, r, r, 6)
            for j in range(2):
                v0[1, x, r, j] = values[j]
    v0[1, pl.ds(1, 1)] = far_low[...]
    v0[1, pl.ds(8, 1)] = far_high[...]
    for x in range(1, 9):
        for r in range(6):
            for j in range(2):
                add = rows_eb[(x - 1) // 2, j, pl.ds(4 + r // 2, SUB, stride=3), :]
                v0[1, x, r, j] = v0[1, x, r, j] + add
    sweep_one()
    swap_last = exchange(last_low, last_high)
    sweep_two(swap_last, last_low, last_high)

    for x in range(3, 7):
        for c in (0, 1):
            for r in range(6):
                b = fine.bit(c, x % 2, r)
                part = fine.residual(c, x, x % 2, r)
                for j in range(2):
                    rows_p[x - 3, 2 * j + b, pl.ds(r, SUB, stride=6), :] = v0[c, x, r, j]
                    rows_a[x, 2 * j + b, pl.ds(r, SUB, stride=6), :] = part[j]
    for x in range(4):
        for t, tile in enumerate(join_lanes([rows_p[x, q, pl.ds(8, 32), :] for q in range(4)])):
            p_vm[x, :, pl.ds(LANES * t, LANES)] = tile
        for t, tile in enumerate(join_lanes([rows_a[x + 3, q, pl.ds(8, 32), :] for q in range(4)])):
            r_vm[x, :, pl.ds(LANES * t, LANES)] = tile
    outs = [
        pltpu.make_async_copy(p_vm, p_out, out_sem.at[0]),
        pltpu.make_async_copy(r_vm, r_out, out_sem.at[1]),
    ]
    for out in outs:
        out.start()
    for group in (phase_first, guess_first, rhs_first, phase_more, rhs_more, m1_blocks, s1_blocks, e1_blocks):
        wire.sent(group)
    m2_all.sent()
    s2_all.sent()
    for out in outs:
        out.wait()


def scratch(ng):
    vec = lambda *shape: pltpu.VMEM(shape + (SUB, LANES), F32)
    rows = lambda *shape: pltpu.VMEM(shape + (LANES,), F32)
    two = ng + 2 * PAD2
    shapes = [pltpu.VMEM((10, 48, 512), jnp.int32), pltpu.VMEM((10, 48, 512), F32), pltpu.VMEM((10, 48, 512), F32)]
    shapes += [rows(10, 4, 48)] * 3
    for n, r, j in ((10, 6, 2), (12, 4, 1)):
        shapes += [vec(2, n, r, j)] * 6 + [vec(2, n, j), vec(2, n, r)] + [vec(2, n, r, j)] * 2
    shapes += [vec(two, 4)] * 6 + [vec(two)] + [vec(two, 4)] * 2
    shapes += [rows(2, 2, 32)] * 3 + [rows(12, 2, 32)] * 3
    shapes += [rows(8), rows(24), rows(two, 40), rows(two, 40), rows(two, 32), rows(4, 2, 32)]
    shapes += [vec(3, 6, 2)] * 4 + [vec(1, 6, 2)] * 2
    shapes += [rows(4, 4, 48)] * 2 + [pltpu.VMEM((4, 32, 512), F32), pltpu.VMEM((4, 32, 512), F32)]
    count = 160
    shapes += [pltpu.SemaphoreType.DMA((3,)), pltpu.SemaphoreType.DMA((2,))]
    shapes += [pltpu.SemaphoreType.DMA((count,)), pltpu.SemaphoreType.DMA((count,))]
    return shapes


def solution(mesh):
    ng, ny = mesh.shape["gx"], mesh.shape["yz"]

    def local(right_side, phase, pressure_guess):
        anywhere = pl.BlockSpec(memory_space=pl.ANY)
        out = jax.ShapeDtypeStruct(right_side.shape, F32)
        return pl.pallas_call(
            functools.partial(kernel, ng, ny),
            out_shape=(out, out),
            in_specs=[anywhere] * 3,
            out_specs=(anywhere, anywhere),
            scratch_shapes=scratch(ng),
            compiler_params=pltpu.CompilerParams(
                collective_id=0, has_side_effects=True, vmem_limit_bytes=56 * 1024 * 1024
            ),
            name="vcycle",
        )(right_side, phase, pressure_guess)

    specs = P("gx", "yz", None)
    return jax.shard_map(
        local, mesh=mesh, in_specs=(specs,) * 3, out_specs=(specs, specs), check_vma=False
    )
```

```python
import functools

import jax
import jax.numpy as jnp
import numpy as np
from jax import lax
from jax.experimental import pallas as pl
from jax.experimental.pallas import tpu as pltpu
from jax.sharding import PartitionSpec as P

MESH = pl.DeviceIdType.MESH
F32 = jnp.float32
LANES = 128
SUB = 8
PAD2 = 3
MIXED = np.float32(2000.0) / np.float32(1001.0)


def lanes_of(shape):
    return lax.broadcasted_iota(jnp.int32, shape, len(shape) - 1)


def roll(value, shift, axis):
    size = value.shape[axis]
    return pltpu.roll(value, shift % size, axis)


def split_lanes(tiles):
    shape = tiles[0].shape
    lane = lanes_of(shape)
    block = lane // 32
    within = lane % 32
    parts = [
        jnp.take_along_axis(tiles[t], 4 * within + (block + 4 - t) % 4, axis=1) for t in range(4)
    ]
    out = []
    for k in range(4):
        pick = parts[(3 - k) % 4]
        for b in (2, 1, 0):
            pick = jnp.where(block == b, parts[(b - k) % 4], pick)
        out.append(pick if k == 0 else roll(pick, -32 * k, 1))
    return out


def join_lanes(quarters):
    shape = quarters[0].shape
    lane = lanes_of(shape)
    block = lane // 32
    turned = [quarters[k] if k == 0 else roll(quarters[k], 32 * k, 1) for k in range(4)]
    out = []
    for t in range(4):
        pick = turned[(3 - t) % 4]
        for b in (2, 1, 0):
            pick = jnp.where(block == b, turned[(b - t) % 4], pick)
        out.append(jnp.take_along_axis(pick, ((lane % 4 + t) % 4) * 32 + lane // 4, axis=1))
    return out


def planes(low, high, body):
    count = high - low
    if count % 2 == 0 and count > 2:

        def pair(i, carry):
            body(low + 2 * i, low % 2)
            body(low + 2 * i + 1, (low + 1) % 2)
            return carry

        lax.fori_loop(0, count // 2, pair, 0)
    else:
        for x in range(low, high):
            body(x, x % 2)


class Level:
    def __init__(self, rows, pairs, refs, face, span=LANES):
        self.rows, self.pairs, self.face = rows, pairs, face
        self.span = span
        self.v, self.s, self.m, self.cx, self.cy, self.cz, self.cyl, self.czl, self.d, self.inv = refs

    def bit(self, c, par, r):
        return (c + par + 1 + r) % 2

    def load(self, ref, x, c, par, r, start, stride):
        b = self.bit(c, par, r)
        return [ref[x, 2 * j + b, pl.ds(start, SUB, stride=stride), :] for j in range(self.pairs)]

    def z_shift_up(self, values, b):
        if b == 0:
            return values
        return values[1:] + [roll(values[0], -1, 1)]

    def z_shift_down(self, values, b):
        if b == 1:
            return values
        return [roll(values[-1], 1, 1)] + values[:-1]

    def get(self, ref, c, x, r):
        return [ref[c, x, r, j] for j in range(self.pairs)]

    def y_up(self, ref, c, x, r):
        if r < self.rows - 1:
            return self.get(ref, c, x, r + 1)
        return [roll(v, -1, 0) for v in self.get(ref, c, x, 0)]

    def y_down(self, ref, c, x, r):
        if r > 0:
            return self.get(ref, c, x, r - 1)
        return [roll(v, 1, 0) for v in self.get(ref, c, x, self.rows - 1)]

    def faces_x(self, low, high):
        def body(x, par):
            for c in (0, 1):
                for r in range(self.rows):
                    here, there = self.get(self.m, c, x, r), self.get(self.m, 1 - c, x + 1, r)
                    for j in range(self.pairs):
                        self.cx[c, x, r, j] = self.face(here[j], there[j])

        planes(low, high, body)

    def faces_yz(self, low, high):
        last = lanes_of((SUB, LANES)) % self.span == self.span - 1

        def body(x, par):
            for c in (0, 1):
                for r in range(self.rows):
                    b = self.bit(c, par, r)
                    here = self.get(self.m, c, x, r)
                    there = self.y_up(self.m, 1 - c, x, r)
                    above = self.z_shift_up(self.get(self.m, 1 - c, x, r), b)
                    for j in range(self.pairs):
                        self.cy[c, x, r, j] = self.face(here[j], there[j])
                        up = self.face(here[j], above[j])
                        if b == 1 and j == self.pairs - 1:
                            up = jnp.where(last, 0.0, up)
                        self.cz[c, x, r, j] = up

        planes(low, high, body)

    def diagonals(self, low, high):
        last = lanes_of((SUB, LANES)) % self.span == self.span - 1

        def body(x, par):
            for c in (0, 1):
                for r in range(self.rows):
                    b = self.bit(c, par, r)
                    xl, xu = self.get(self.cx, 1 - c, x - 1, r), self.get(self.cx, c, x, r)
                    yl, yu = self.y_down(self.cy, 1 - c, x, r), self.get(self.cy, c, x, r)
                    zl = self.z_shift_down(self.get(self.cz, 1 - c, x, r), b)
                    zu = self.get(self.cz, c, x, r)
                    for j in range(self.pairs):
                        if r == 0:
                            self.cyl[c, x, j] = yl[j]
                        if b == 0 and j == 0:
                            self.czl[c, x, r] = zl[j]
                        total = xl[j] + xu[j] + yl[j] + yu[j] + zl[j] + zu[j]
                        if b == 1 and j == self.pairs - 1:
                            total = total + jnp.where(last, 2.0 * self.m[c, x, r, j], 0.0)
                        total = jnp.where(total > 0, total, 1.0)
                        self.d[c, x, r, j] = total
                        self.inv[c, x, r, j] = 1.0 / total

        planes(low, high, body)

    def beside(self, c, x, par, r):
        o = 1 - c
        b = self.bit(c, par, r)
        same = self.get(self.v, o, x, r)
        parts = [
            (self.get(self.cx, o, x - 1, r), self.get(self.v, o, x - 1, r)),
            (self.get(self.cx, c, x, r), self.get(self.v, o, x + 1, r)),
            (
                self.get(self.cy, o, x, r - 1) if r else [self.cyl[c, x, j] for j in range(self.pairs)],
                self.y_down(self.v, o, x, r),
            ),
            (self.get(self.cy, c, x, r), self.y_up(self.v, o, x, r)),
        ]
        lower = self.get(self.cz, o, x, r)
        if b == 0:
            lower = [self.czl[c, x, r]] + lower[:-1]
        parts.append((lower, self.z_shift_down(same, b)))
        parts.append((self.get(self.cz, c, x, r), self.z_shift_up(same, b)))
        out = []
        for j in range(self.pairs):
            terms = [k[j] * v[j] for k, v in parts]
            out.append((terms[0] + terms[1]) + (terms[2] + terms[3]) + (terms[4] + terms[5]))
        return out

    def colour_pass(self, c, low, high):
        def body(x, par):
            for r in range(self.rows):
                total = self.beside(c, x, par, r)
                for j in range(self.pairs):
                    self.v[c, x, r, j] = (self.s[c, x, r, j] + total[j]) * self.inv[c, x, r, j]

        planes(low, high, body)

    def residual(self, c, x, par, r):
        total = self.beside(c, x, par, r)
        return [
            self.s[c, x, r, j] - (self.d[c, x, r, j] * self.v[c, x, r, j] - total[j])
            for j in range(self.pairs)
        ]


def face_fine(left, right):
    both = left * right
    return jnp.where(both > 1e5, 1000.0, jnp.where(both > 500.0, MIXED, both))


def face_coarse(left, right):
    return 2.0 * left * right / jnp.maximum(left + right, 0.5)


class Wire:
    def __init__(self, ng, ny, send, recv):
        self.ng, self.ny, self.send, self.recv, self.used = ng, ny, send, recv, 0
        self.g, self.y = lax.axis_index("gx"), lax.axis_index("yz")
        self.coming, self.going, self.gathers = [], [], []

    def inside(self, dg, dy):
        g, y = self.g + dg, self.y + dy
        return (g >= 0) & (g < self.ng) & (y >= 0) & (y < self.ny)

    def copy(self, src, dst, dg, dy):
        k = self.used
        self.used += 1
        made = pltpu.make_async_remote_copy(
            src_ref=src,
            dst_ref=dst,
            send_sem=self.send.at[k],
            recv_sem=self.recv.at[k],
            device_id=(self.g + dg, self.y + dy),
            device_id_type=MESH,
        )
        return (made, dst, dg, dy)

    def start(self, copies):
        for made, _, dg, dy in copies:
            pl.when(self.inside(dg, dy))(made.start)
        self.coming += copies
        self.going += copies

    def arrive(self, copies, fill=0):
        for made, dst, dg, dy in copies:
            there = self.inside(-dg, -dy)
            pl.when(there)(made.wait_recv)
            self.coming = [c for c in self.coming if c[0] is not made]
            if fill is not None:

                @pl.when(jnp.logical_not(there))
                def _(dst=dst):
                    dst[...] = jnp.full(dst.shape, fill, dst.dtype)

    def sent(self, copies):
        for made, _, dg, dy in copies:
            pl.when(self.inside(dg, dy))(made.wait_send)
            self.going = [c for c in self.going if c[0] is not made]

    def drain(self):
        self.arrive(list(self.coming), None)
        self.sent(list(self.going))
        for gather in self.gathers:
            gather.sent()


def fine_planes(wire, src, dst, low, high):
    n = high - low
    rows = pl.ds(8, 32)
    return [
        wire.copy(src.at[pl.ds(4 - high, n)], dst.at[pl.ds(3 - high, n), rows, :], 1, 0),
        wire.copy(src.at[pl.ds(low, n)], dst.at[pl.ds(7 + low, n), rows, :], -1, 0),
    ]


def fine_rims(wire, src, dst):
    own = pl.ds(3, 4)
    return [
        wire.copy(src.at[:, pl.ds(24, 8), :], dst.at[own, pl.ds(0, 8), :], 0, 1),
        wire.copy(src.at[:, pl.ds(0, 8), :], dst.at[own, pl.ds(40, 8), :], 0, -1),
    ]


def fine_corners(wire, ref, spans):
    out = []
    for first, n in spans:
        xs = pl.ds(first, n)
        out.append(wire.copy(ref.at[xs, pl.ds(32, 8), :], ref.at[xs, pl.ds(0, 8), :], 0, 1))
        out.append(wire.copy(ref.at[xs, pl.ds(8, 8), :], ref.at[xs, pl.ds(40, 8), :], 0, -1))
    return out


def middle_blocks(wire, src, dst, reach, sides=(-1, 0, 1)):
    out = []
    for dg in range(-3, 4):
        for dy in sides:
            if (dg, dy) == (0, 0) or 2 * abs(dg) - 1 > reach:
                continue
            if abs(dg) == 3:
                xs, xd = (pl.ds(1, 1), pl.ds(0, 1)) if dg == 3 else (pl.ds(0, 1), pl.ds(11, 1))
            else:
                xs, xd = pl.ds(0, 2), pl.ds(5 - 2 * dg, 2)
            ys, yd = ((8, 8), (24, 8)) if dy == -1 else ((16, 8), (0, 8)) if dy == 1 else ((8, 16), (8, 16))
            out.append(
                wire.copy(src.at[xs, :, pl.ds(*ys), :], dst.at[xd, :, pl.ds(*yd), :], dg, dy)
            )
    return out


def middle_corners(wire, ref):
    return [
        wire.copy(ref.at[:, :, pl.ds(16, 8), :], ref.at[:, :, pl.ds(0, 8), :], 0, 1),
        wire.copy(ref.at[:, :, pl.ds(8, 8), :], ref.at[:, :, pl.ds(24, 8), :], 0, -1),
    ]


class Gather:
    def __init__(self, wire, src, dst):
        self.wire, self.src, self.dst = wire, src, dst
        self.first = wire.used
        self.n = wire.ng
        wire.used += self.n
        self.rows = pl.ds(16, 8)
        self.along, self.landed = [], False

    def hop(self, d, plane):
        wire = self.wire
        return pltpu.make_async_remote_copy(
            src_ref=self.src,
            dst_ref=self.dst.at[plane, self.rows, :],
            send_sem=wire.send.at[self.first + d],
            recv_sem=wire.recv.at[self.first + plane],
            device_id=((wire.g + d) % self.n, wire.y),
            device_id_type=MESH,
        )

    def start(self):
        self.wire.gathers.append(self)
        for d in range(1, self.n):
            self.hop(d, self.wire.g).start()

    def forward(self):
        wire, n = self.wire, self.n
        self.landed = True
        groups = n // 4
        for k in sorted(range(groups), key=lambda k: min(k, groups - k)):
            base = 4 * ((wire.g // 4 + k) % groups)
            for i in range(4):
                pl.when(base + i != wire.g)(self.hop(1, base + i).wait_recv)
            span = pl.ds(base, 4)
            made = [
                wire.copy(
                    self.dst.at[span, self.rows, :],
                    self.dst.at[span, pl.ds(16 - 8 * dy, 8), :],
                    0,
                    dy,
                )
                for dy in (-2, 2, -1, 1)
            ]
            wire.start(made)
            self.along += made

    def finish(self):
        self.wire.arrive(self.along)

    def sent(self):
        for d in range(1, self.n):
            self.hop(d, self.wire.g).wait_send()


def kernel(
    ng, ny,
    rhs, phase, guess, p_out, r_out,
    in_phase, in_guess, in_rhs, rows_a, rows_b, rows_c,
    v0, s0, m0, cx0, cy0, cz0, cyl0, czl0, d0, inv0,
    v1, s1, m1, cx1, cy1, cz1, cyl1, czl1, d1, inv1,
    v2, s2, m2, cx2, cy2, cz2, cyl2, czl2, d2, inv2,
    send_m1, send_s1, send_e1, wide_m1, wide_s1, wide_e1,
    send_m2, send_s2, rows_s2, wide_m2, wide_s2, rows_e2, rows_eb,
    got_low, got_high, last_low, last_high, far_low, far_high,
    rows_p, rows_far, p_vm, r_vm,
    local, out_sem, send, recv,
):
    wire = Wire(ng, ny, send, recv)
    for _ in stages(
        wire, ng,
    rhs, phase, guess, p_out, r_out,
    in_phase, in_guess, in_rhs, rows_a, rows_b, rows_c,
    v0, s0, m0, cx0, cy0, cz0, cyl0, czl0, d0, inv0,
    v1, s1, m1, cx1, cy1, cz1, cyl1, czl1, d1, inv1,
    v2, s2, m2, cx2, cy2, cz2, cyl2, czl2, d2, inv2,
    send_m1, send_s1, send_e1, wide_m1, wide_s1, wide_e1,
    send_m2, send_s2, rows_s2, wide_m2, wide_s2, rows_e2, rows_eb,
    got_low, got_high, last_low, last_high, far_low, far_high,
    rows_p, rows_far, p_vm, r_vm,
    local, out_sem,
    ):
        pass
    wire.drain()


def stages(
    wire, ng,
    rhs, phase, guess, p_out, r_out,
    in_phase, in_guess, in_rhs, rows_a, rows_b, rows_c,
    v0, s0, m0, cx0, cy0, cz0, cyl0, czl0, d0, inv0,
    v1, s1, m1, cx1, cy1, cz1, cyl1, czl1, d1, inv1,
    v2, s2, m2, cx2, cy2, cz2, cyl2, czl2, d2, inv2,
    send_m1, send_s1, send_e1, wide_m1, wide_s1, wide_e1,
    send_m2, send_s2, rows_s2, wide_m2, wide_s2, rows_e2, rows_eb,
    got_low, got_high, last_low, last_high, far_low, far_high,
    rows_p, rows_far, p_vm, r_vm,
    local, out_sem,
):
    g, y = wire.g, wire.y
    fine = Level(6, 2, (v0, s0, m0, cx0, cy0, cz0, cyl0, czl0, d0, inv0), face_fine)
    low = Level(4, 1, (v2, s2, m2, cx2, cy2, cz2, cyl2, czl2, d2, inv2), face_coarse, LANES // 2)
    mid = Level(4, 1, (v1, s1, m1, cx1, cy1, cz1, cyl1, czl1, d1, inv1), face_coarse)

    own = (pl.ds(3, 4), pl.ds(8, 32))
    loads = [
        pltpu.make_async_copy(src, dst.at[own[0], own[1], :], local.at[i])
        for i, (src, dst) in enumerate(((phase, in_phase), (guess, in_guess), (rhs, in_rhs)))
    ]
    for load in loads:
        load.start()

    barrier = pltpu.get_barrier_semaphore()
    peers = [(dg, dy) for dg in range(-2, 3) for dy in (-1, 0, 1) if dy != 0 or dg == 0]
    peers = [p for p in peers if p != (0, 0)] + [(0, -2), (0, 2)]
    count = jnp.int32(ng - 1)
    for dg, dy in peers:
        there = wire.inside(dg, dy)
        count = count + there.astype(jnp.int32)

        @pl.when(there)
        def _(dg=dg, dy=dy):
            pl.semaphore_signal(barrier, inc=1, device_id=(g + dg, y + dy), device_id_type=MESH)

    for d in range(1, ng):
        pl.semaphore_signal(barrier, inc=1, device_id=((g + d) % ng, y), device_id_type=MESH)
    pl.semaphore_wait(barrier, count)

    yield
    phase_rims, guess_rims, rhs_rims = [
        fine_rims(wire, src, dst)
        for src, dst in ((phase, in_phase), (guess, in_guess), (rhs, in_rhs))
    ]
    phase_first = fine_planes(wire, phase, in_phase, 0, 2)
    phase_more = fine_planes(wire, phase, in_phase, 2, 3)
    for group in (phase_first, guess_rims, rhs_rims, phase_rims, phase_more):
        wire.start(group)

    def unpack(src, dst, low, high, first, count):
        rows = pl.ds(first, count)

        def body(x, carry):
            tiles = [src[x, rows, pl.ds(LANES * t, LANES)] for t in range(4)]
            for q, part in enumerate(split_lanes(tiles)):
                dst[x, q, rows, :] = part
            return carry

        lax.fori_loop(low, high, body, 0)

    def unpack_phase(low, high, first, count):
        rows = pl.ds(first, count)

        def body(x, carry):
            tiles = []
            for t in range(4):
                tile = in_phase[x, rows, pl.ds(LANES * t, LANES)]
                value = jnp.where(tile > 0, 1000.0, 1.0)
                tiles.append(jnp.where(tile < 0, 0.0, value))
            for q, part in enumerate(split_lanes(tiles)):
                rows_a[x, q, rows, :] = part
            return carry

        lax.fori_loop(low, high, body, 0)

    def dense(ref, rows, low, high, colours):
        def body(x, par):
            for c in colours:
                for r in range(6):
                    values = fine.load(rows, x, c, par, r, r, 6)
                    for j in range(2):
                        ref[c, x, r, j] = values[j]

        planes(low, high, body)

    yield
    loads[1].wait()
    wire.arrive(guess_rims)
    unpack(in_guess, rows_b, 3, 7, 0, 48)
    dense(v0, rows_b, 3, 7, (1,))
    guess_first = [
        wire.copy(v0.at[1, pl.ds(5, 2)], v0.at[1, pl.ds(1, 2)], 1, 0),
        wire.copy(v0.at[1, pl.ds(3, 2)], v0.at[1, pl.ds(7, 2)], -1, 0),
    ]
    wire.start(guess_first)
    loads[2].wait()
    wire.arrive(rhs_rims)
    unpack(in_rhs, rows_c, 3, 7, 0, 48)
    dense(s0, rows_c, 3, 7, (0, 1))
    rhs_first = [
        wire.copy(s0.at[0, 6], s0.at[0, 2], 1, 0),
        wire.copy(s0.at[0, 3], s0.at[0, 7], -1, 0),
    ]
    rhs_more = [
        wire.copy(s0.at[1, 6], s0.at[1, 2], 1, 0),
        wire.copy(s0.at[1, 3], s0.at[1, 7], -1, 0),
        wire.copy(s0.at[0, 5], s0.at[0, 1], 1, 0),
        wire.copy(s0.at[0, 4], s0.at[0, 8], -1, 0),
    ]
    wire.start(rhs_first)
    wire.start(rhs_more)

    lane = lanes_of((SUB, LANES))
    left = lane < LANES // 2
    pack = jnp.where(left, 2 * lane, 2 * lane - (LANES - 1))
    loads[0].wait()
    unpack_phase(3, 7, 8, 32)
    coarsest = None
    for big in range(2):
        for q in range(2):
            for half in range(2):
                total = None
                for x in (3 + 2 * big, 4 + 2 * big):
                    for k in (0, 1):
                        for r in (2 * half, 2 * half + 1):
                            part = rows_a[x, 2 * q + k, pl.ds(8 + r, SUB, stride=4), :]
                            total = part if total is None else total + part
                total = 0.125 * total
                send_m1[big, q, pl.ds(8 + half, SUB, stride=2), :] = total
                coarsest = total if coarsest is None else coarsest + total
    coarsest = jnp.take_along_axis(0.125 * coarsest, pack, axis=1)
    send_m2[...] = coarsest
    m1_blocks = middle_blocks(wire, send_m1, wide_m1, 5, (0,))
    wire.start(m1_blocks)
    m2_all = Gather(wire, send_m2, wide_m2)
    m2_all.start()
    wide_m2[g, pl.ds(16, 8), :] = coarsest
    wide_m1[pl.ds(5, 2), :, pl.ds(8, 16), :] = send_m1[:, :, pl.ds(8, 16), :]
    wire.arrive(phase_rims, -1)
    unpack_phase(3, 7, 0, 8)
    unpack_phase(3, 7, 40, 8)

    wire.arrive(phase_first, -1)
    corners_first = fine_corners(wire, in_phase, ((1, 2), (7, 2)))
    wire.start(corners_first)
    unpack_phase(1, 3, 8, 32)
    unpack_phase(7, 9, 8, 32)
    wire.arrive(phase_more, -1)
    corners_more = fine_corners(wire, in_phase, ((0, 1), (9, 1)))
    wire.start(corners_more)
    yield
    wire.arrive(corners_first, -1)
    for first in (0, 40):
        unpack_phase(1, 3, first, 8)
        unpack_phase(7, 9, first, 8)
    dense(m0, rows_a, 1, 9, (0, 1))
    fine.faces_x(1, 8)
    fine.faces_yz(2, 8)
    fine.diagonals(2, 8)
    yield
    wire.arrive(guess_first)
    wire.arrive(rhs_first)
    yield

    def sweep_one(waiting=()):
        fine.colour_pass(0, 2, 8)
        wire.sent(waiting)
        fine.colour_pass(1, 3, 7)

    def exchange(low, high):
        copies = [
            wire.copy(v0.at[1, pl.ds(4, 3)], low, 1, 0),
            wire.copy(v0.at[1, pl.ds(3, 3)], high, -1, 0),
        ]
        wire.start(copies)
        return copies

    def sweep_two(copies, low, high):
        wire.arrive(copies)
        v0[1, pl.ds(0, 3)] = low[...]
        v0[1, pl.ds(7, 3)] = high[...]
        fine.colour_pass(0, 1, 9)
        wire.sent(copies)
        fine.colour_pass(1, 2, 8)

    sweep_one(guess_first)
    yield
    swap = exchange(got_low, got_high)
    wire.arrive(m1_blocks)
    m1_corners = middle_corners(wire, wide_m1)
    wire.start(m1_corners)
    m2_all.forward()
    wire.arrive(corners_more, -1)
    unpack_phase(0, 1, 0, 48)
    unpack_phase(9, 10, 0, 48)
    dense(m0, rows_a, 0, 1, (0, 1))
    dense(m0, rows_a, 9, 10, (0, 1))
    fine.faces_x(0, 1)
    fine.faces_x(8, 9)
    fine.faces_yz(1, 2)
    fine.faces_yz(8, 9)
    fine.diagonals(1, 2)
    fine.diagonals(8, 9)
    wire.arrive(rhs_more)
    yield
    sweep_two(swap, got_low, got_high)

    yield
    for big in range(2):
        for r1 in range(3):
            total = [None, None]
            for x in (3 + 2 * big, 4 + 2 * big):
                for r in (2 * r1, 2 * r1 + 1):
                    for c in (0, 1):
                        part = fine.residual(c, x, x % 2, r)
                        for j in range(2):
                            total[j] = part[j] if total[j] is None else total[j] + part[j]
            for j in range(2):
                send_s1[big, j, pl.ds(4 + r1, SUB, stride=3), :] = 0.5 * total[j]
    s1_blocks = middle_blocks(wire, send_s1, wide_s1, 4)
    wire.start(s1_blocks)
    wide_s1[pl.ds(5, 2), :, pl.ds(8, 16), :] = send_s1[:, :, pl.ds(8, 16), :]

    yield
    for x in range(3, 7):
        for c in (0, 1):
            for r in range(6):
                b = fine.bit(c, x % 2, r)
                for j in range(2):
                    rows_p[x - 3, 2 * j + b, pl.ds(r, SUB, stride=6), :] = v0[c, x, r, j]
    far = [
        wire.copy(v0.at[1, pl.ds(5, 1)], far_low, 1, 0),
        wire.copy(v0.at[1, pl.ds(4, 1)], far_high, -1, 0),
        wire.copy(rows_p.at[:, :, pl.ds(32, 8), :], rows_far.at[:, :, pl.ds(0, 8), :], 0, 1),
        wire.copy(rows_p.at[:, :, pl.ds(8, 8), :], rows_far.at[:, :, pl.ds(40, 8), :], 0, -1),
    ]
    wire.start(far)

    yield
    wire.arrive(m1_corners)

    def dense_mid(ref, rows, low, high, colours):
        def body(x, par):
            for c in colours:
                for r in range(4):
                    ref[c, x, r, 0] = mid.load(rows, x, c, par, r, r, 4)[0]

        planes(low, high, body)

    dense_mid(m1, wide_m1, 0, 12, (0, 1))
    mid.faces_x(0, 11)
    mid.faces_yz(1, 11)
    mid.diagonals(1, 11)
    v1[1] = jnp.zeros(v1.shape[1:], F32)

    def sweeps_mid():
        mid.colour_pass(0, 1, 11)
        mid.colour_pass(1, 2, 10)
        mid.colour_pass(0, 3, 9)
        mid.colour_pass(1, 4, 8)

    yield
    wire.arrive(s1_blocks)
    yield
    dense_mid(s1, wide_s1, 1, 11, (0, 1))
    sweeps_mid()
    for r2 in range(2):
        total = None
        for x in (5, 6):
            for r in (2 * r2, 2 * r2 + 1):
                for c in (0, 1):
                    part = mid.residual(c, x, x % 2, r)[0]
                    total = part if total is None else total + part
        rows_s2[pl.ds(4 + r2, SUB, stride=2), :] = 0.5 * total
    send_s2[...] = jnp.take_along_axis(rows_s2[pl.ds(8, 8), :], pack, axis=1)
    yield
    s2_all = Gather(wire, send_s2, wide_s2)
    s2_all.start()
    wide_s2[g, pl.ds(16, 8), :] = send_s2[...]
    for x in (5, 6):
        for c in (0, 1):
            for r in range(4):
                b = mid.bit(c, x % 2, r)
                send_e1[x - 5, b, pl.ds(r, SUB, stride=4), :] = v1[c, x, r, 0]
    e1_blocks = middle_blocks(wire, send_e1, wide_e1, 5, (0,))
    wire.start(e1_blocks)
    wide_e1[pl.ds(5, 2), :, pl.ds(8, 16), :] = send_e1[:, :, pl.ds(8, 16), :]

    yield
    m2_all.finish()
    half = ng // 2

    def load_low(ref, rows):
        def body(x, par):
            for r in range(4):
                at = pl.ds(4 + r, SUB, stride=4)
                one, two = rows[x - 1, at, :], rows[x - 1 + half, at, :]
                even = jnp.where(left, one, roll(two, LANES // 2, 1))
                odd = jnp.where(left, roll(one, LANES // 2, 1), two)
                for c in (0, 1):
                    ref[c, x, r, 0] = odd if low.bit(c, par, r) else even

        planes(1, half + 1, body)

    load_low(m2, wide_m2)
    for c in (0, 1):
        for r in range(4):
            m2[c, 0, r, 0] = jnp.where(left, 0.0, roll(m2[c, half, r, 0], LANES // 2, 1))
            m2[c, half + 1, r, 0] = jnp.where(left, roll(m2[c, 1, r, 0], LANES // 2, 1), 0.0)
    v2[1] = jnp.zeros(v2.shape[1:], F32)
    low.faces_x(0, half + 1)
    low.faces_yz(1, half + 1)
    low.diagonals(1, half + 1)
    yield
    s2_all.forward()
    wire.arrive(e1_blocks)
    e1_corners = middle_corners(wire, wide_e1)
    wire.start(e1_corners)
    yield
    s2_all.finish()
    yield
    load_low(s2, wide_s2)

    def pass_low(c):
        for r in range(4):
            v2[1 - c, 0, r, 0] = roll(v2[1 - c, half, r, 0], LANES // 2, 1)
            v2[1 - c, half + 1, r, 0] = roll(v2[1 - c, 1, r, 0], LANES // 2, 1)
        low.colour_pass(c, 1, half + 1)

    def sweep_low(i, carry):
        pass_low(0)
        pass_low(1)
        return carry

    lax.fori_loop(0, 4, sweep_low, 0)
    yield
    natural = (lane % 2) * (LANES // 2) + lane // 2

    def keep_low(x, par):
        for r in range(4):
            parts = [v2[c, x, r, 0] for c in (0, 1)]
            even, odd = parts if low.bit(0, par, r) == 0 else parts[::-1]
            at = pl.ds(r, SUB, stride=4)
            one = jnp.where(left, even, roll(odd, LANES // 2, 1))
            two = jnp.where(left, roll(even, LANES // 2, 1), odd)
            rows_e2[PAD2 + x - 1, at, :] = jnp.take_along_axis(one, natural, axis=1)
            rows_e2[PAD2 + x - 1 + half, at, :] = jnp.take_along_axis(two, natural, axis=1)

    planes(1, half + 1, keep_low)
    for x in range(PAD2):
        rows_e2[x] = jnp.zeros((32, LANES), F32)
        rows_e2[PAD2 + ng + x] = jnp.zeros((32, LANES), F32)

    yield
    wire.arrive(e1_corners)
    for x in range(12):
        source = g + ((x + 1) // 2 - 3 + PAD2)
        for r in range(4):
            value = mid.load(wide_e1, x, 1, x % 2, r, r, 4)[0]
            v1[1, x, r, 0] = value + rows_e2[source, pl.ds(8 + r // 2, SUB, stride=2), :]
    sweeps_mid()
    for x in range(4, 8):
        for c in (0, 1):
            for r in range(4):
                b = mid.bit(c, x % 2, r)
                rows_eb[x - 4, b, pl.ds(r, SUB, stride=4), :] = v1[c, x, r, 0]

    yield
    wire.arrive(far[2:])
    wire.arrive(far[:2])
    wire.sent(far)
    rows_far[:, :, pl.ds(8, 32), :] = rows_p[:, :, pl.ds(8, 32), :]
    for x in range(3, 7):
        for r in range(6):
            values = fine.load(rows_far, x - 3, 1, x % 2, r, r, 6)
            for j in range(2):
                v0[1, x, r, j] = values[j]
    v0[1, pl.ds(1, 1)] = far_low[...]
    v0[1, pl.ds(8, 1)] = far_high[...]
    for x in range(1, 9):
        for r in range(6):
            for j in range(2):
                add = rows_eb[(x - 1) // 2, j, pl.ds(4 + r // 2, SUB, stride=3), :]
                v0[1, x, r, j] = v0[1, x, r, j] + add
    yield
    sweep_one()
    swap_last = exchange(last_low, last_high)
    yield
    sweep_two(swap_last, last_low, last_high)

    yield
    for x in range(3, 7):
        for c in (0, 1):
            for r in range(6):
                b = fine.bit(c, x % 2, r)
                part = fine.residual(c, x, x % 2, r)
                for j in range(2):
                    rows_p[x - 3, 2 * j + b, pl.ds(r, SUB, stride=6), :] = v0[c, x, r, j]
                    rows_a[x, 2 * j + b, pl.ds(r, SUB, stride=6), :] = part[j]
    for x in range(4):
        for t, tile in enumerate(join_lanes([rows_p[x, q, pl.ds(8, 32), :] for q in range(4)])):
            p_vm[x, :, pl.ds(LANES * t, LANES)] = tile
        for t, tile in enumerate(join_lanes([rows_a[x + 3, q, pl.ds(8, 32), :] for q in range(4)])):
            r_vm[x, :, pl.ds(LANES * t, LANES)] = tile
    outs = [
        pltpu.make_async_copy(p_vm, p_out, out_sem.at[0]),
        pltpu.make_async_copy(r_vm, r_out, out_sem.at[1]),
    ]
    for out in outs:
        out.start()
    for out in outs:
        out.wait()


def scratch(ng):
    vec = lambda *shape: pltpu.VMEM(shape + (SUB, LANES), F32)
    rows = lambda *shape: pltpu.VMEM(shape + (LANES,), F32)
    two = ng + 2 * PAD2
    shapes = [pltpu.VMEM((10, 48, 512), jnp.int32), pltpu.VMEM((10, 48, 512), F32), pltpu.VMEM((10, 48, 512), F32)]
    shapes += [rows(10, 4, 48)] * 3
    for n, r, j in ((10, 6, 2), (12, 4, 1), (ng // 2 + 2, 4, 1)):
        shapes += [vec(2, n, r, j)] * 6 + [vec(2, n, j), vec(2, n, r)] + [vec(2, n, r, j)] * 2
    shapes += [rows(2, 2, 32)] * 3 + [rows(12, 2, 32)] * 3
    shapes += [rows(8), rows(8), rows(24), rows(ng, 40), rows(ng, 40), rows(two, 32), rows(4, 2, 32)]
    shapes += [vec(3, 6, 2)] * 4 + [vec(1, 6, 2)] * 2
    shapes += [rows(4, 4, 48)] * 2 + [pltpu.VMEM((4, 32, 512), F32), pltpu.VMEM((4, 32, 512), F32)]
    count = 160
    shapes += [pltpu.SemaphoreType.DMA((3,)), pltpu.SemaphoreType.DMA((2,))]
    shapes += [pltpu.SemaphoreType.DMA((count,)), pltpu.SemaphoreType.DMA((count,))]
    return shapes


def solution(mesh):
    ng, ny = mesh.shape["gx"], mesh.shape["yz"]

    def local(right_side, phase, pressure_guess):
        anywhere = pl.BlockSpec(memory_space=pl.ANY)
        out = jax.ShapeDtypeStruct(right_side.shape, F32)
        return pl.pallas_call(
            functools.partial(kernel, ng, ny),
            out_shape=(out, out),
            in_specs=[anywhere] * 3,
            out_specs=(anywhere, anywhere),
            scratch_shapes=scratch(ng),
            compiler_params=pltpu.CompilerParams(
                collective_id=0, has_side_effects=True, vmem_limit_bytes=56 * 1024 * 1024
            ),
            name="vcycle",
        )(right_side, phase, pressure_guess)

    specs = P("gx", "yz", None)
    return jax.shard_map(
        local, mesh=mesh, in_specs=(specs,) * 3, out_specs=(specs, specs), check_vma=False
    )
```
